512 devices in a mesh: shell: 8 (over z), row: 4 (over x_hi, core), col: 16 (over x_lo, y).
Axes of the slice: x: 4 (x_hi: 2, x_lo: 2; x = x_hi * 2 + x_lo), y: 8, z: 8, core: 2. Of those that a mesh axis runs over, the one named last changes fastest.
Arguments:
- left_basis: bfloat16 [2, 4096, 6144], P(None, 'row', 'shell'), may hold values from -6 to 6
- right_basis: bfloat16 [2, 6144, 8192], P(None, 'shell', 'col'), may hold values from -0.078125 to 0.078125
- point_weight: float32 [6144], P('shell'), may hold values from 0.3 to 3
- shell_index: int32 [6144], P('shell'), may hold values from 0 to 11
- green_table: float32 [12, 2], replicated, may hold values from -4 to 4
- pivot_rows: int32 [512], replicated, may hold values from 0 to 4095, as said below
- diag_inverse: bfloat16 [2, 512, 512], replicated, may hold values from -0.005859375 to 0.005859375
Outputs:
- factored: float32 [2, 4, 8, 128, 8192], P(None, 'row', 'shell', None, 'col')
The draws below stay inside these ranges and needn't reach their ends.
Inputs may be any that keep to these rules, and one draw needn't show every extreme that they name: `pivot_rows`: 512 distinct matrix rows.
All inputs are finite; a program needn't handle non-finite values.
Results may differ from the reference program's by a relative error of at most 0.0056.
Values may be sent and summed in bfloat16 or wider, within the bound.
No kernel may reach another device: no remote copies, remote signals or barrier semaphores. Data moves between devices by JAX's collectives and lax.ppermute only.
A program may use at most 128 MiB of HBM per device.

```python
import math
import jax
import jax.numpy as jnp
from jax import lax

W = 512
NK = 12
B = 128
MROWS = 4096
NCOLS = 8192
QTOT = 6144
N_SHELL = 8
N_ROW = 4


def draw_pivot_rows(key, part):
    first_key, second_key = jax.random.split(jax.random.fold_in(key, 7))
    middle_rows = jax.random.permutation(first_key, MROWS - 2)[:W - 2].astype(jnp.int32) + 1
    all_rows = jnp.concatenate([jnp.array([0, MROWS - 1], jnp.int32), middle_rows])
    shuffled = jax.random.permutation(second_key, W)
    return all_rows[shuffled].astype(jnp.int32)


def set_ends(entries, rng, least, top_value):
    longest = entries.shape.index(max(entries.shape))
    spots = []
    for shift in (0, 1):
        where = [jax.random.randint(jax.random.fold_in(rng, axis), (), 0, length) for axis, length in enumerate(entries.shape)]
        where[longest] = (where[longest] + shift) % entries.shape[longest]
        spots.append(tuple(where))
    return entries.at[spots[0]].set(least).at[spots[1]].set(top_value)


def block_scale(rng, dims, shards, least, high):
    def one(dim, blocks):
        steps = jax.random.uniform(jax.random.fold_in(jax.random.fold_in(rng, 6), dim), (blocks,), jnp.float32, least / len(shards), high / len(shards))
        return jnp.repeat(jnp.exp(steps), dims[dim] // blocks).reshape((-1,) + (1,) * (len(dims) - dim - 1))

    loudness = one(*shards[0])
    for cut in shards[1:]:
        loudness = loudness * one(*cut)
    return loudness


def normal_values(rng, dims, width, reach, cuts=(), kind=jnp.bfloat16):
    values = jax.random.normal(rng, dims, jnp.float32) * width
    if len(cuts) > 0:
        values = block_scale(rng, dims, cuts, -0.22, 0.18) * values
    return jnp.clip(values, min=-reach, max=reach).astype(kind)


def setup_inputs(seed: int = 0) -> dict:
    key_list = jax.random.split(jax.random.key(seed), 8)
    left_basis = normal_values(key_list[0], (2, MROWS, QTOT), 1.0, 6.0, ((1, 4), (2, 8)))
    right_basis = normal_values(key_list[1], (2, QTOT, NCOLS), QTOT ** -0.5, 0.078125, ((1, 8), (2, 16)))
    point_weight = jnp.clip(jnp.exp(math.log(3.0) - 2.3025851 * jax.random.uniform(key_list[2], (QTOT,), jnp.float32) ** block_scale(key_list[2], (QTOT,), ((0, 8),), -0.2, 0.2)), 0.3, 3.0)
    shell_index = set_ends(jax.random.randint(key_list[3], (QTOT,), 0, NK), jax.random.fold_in(key_list[3], 1), 0, NK - 1).astype(jnp.int32)
    green_table = normal_values(key_list[4], (NK, 2), 1.0, 4.0, (), jnp.float32)
    pivot_rows = draw_pivot_rows(jax.random.fold_in(key_list[7], 71), 0)
    diag_inverse = normal_values(key_list[6], (2, W, W), (0.5 / W), 0.005859375)
    return dict(left_basis=left_basis, right_basis=right_basis, point_weight=point_weight, shell_index=shell_index, green_table=green_table, pivot_rows=pivot_rows, diag_inverse=diag_inverse)


def reference(left_basis, right_basis, point_weight, shell_index, green_table, pivot_rows, diag_inverse):
    green_real = green_table[shell_index, 0]
    green_imag = green_table[shell_index, 1]
    weight_real = point_weight * green_real
    weight_imag = point_weight * green_imag
    basis_real = right_basis[0].astype(jnp.float32)
    basis_imag = right_basis[1].astype(jnp.float32)
    weighted_real = (weight_real[:, None] * basis_real - weight_imag[:, None] * basis_imag).astype(jnp.bfloat16)
    weighted_imag = (weight_real[:, None] * basis_imag + weight_imag[:, None] * basis_real).astype(jnp.bfloat16)
    coupling_real = jnp.dot(left_basis[0], weighted_real, preferred_element_type=jnp.float32) - jnp.dot(left_basis[1], weighted_imag, preferred_element_type=jnp.float32)
    coupling_imag = jnp.dot(left_basis[0], weighted_imag, preferred_element_type=jnp.float32) + jnp.dot(left_basis[1], weighted_real, preferred_element_type=jnp.float32)
    pivot_real = coupling_real[pivot_rows].astype(jnp.bfloat16)
    pivot_imag = coupling_imag[pivot_rows].astype(jnp.bfloat16)
    panel_real = coupling_real[:, :W]
    panel_imag = coupling_imag[:, :W]
    inverse_real = diag_inverse[0].astype(jnp.float32)
    inverse_imag = diag_inverse[1].astype(jnp.float32)
    highest = lax.Precision.HIGHEST
    mult_real = (jnp.dot(panel_real, inverse_real, precision=highest, preferred_element_type=jnp.float32) - jnp.dot(panel_imag, inverse_imag, precision=highest, preferred_element_type=jnp.float32)).astype(jnp.bfloat16)
    mult_imag = (jnp.dot(panel_real, inverse_imag, precision=highest, preferred_element_type=jnp.float32) + jnp.dot(panel_imag, inverse_real, precision=highest, preferred_element_type=jnp.float32)).astype(jnp.bfloat16)
    update_real = jnp.dot(mult_real, pivot_real, preferred_element_type=jnp.float32) - jnp.dot(mult_imag, pivot_imag, preferred_element_type=jnp.float32)
    update_imag = jnp.dot(mult_real, pivot_imag, preferred_element_type=jnp.float32) + jnp.dot(mult_imag, pivot_real, preferred_element_type=jnp.float32)
    updated = jnp.stack([coupling_real - update_real, coupling_imag - update_imag])
    return updated.reshape(2, N_ROW, N_SHELL, B, NCOLS)
```

```python
import jax
import jax.numpy as jnp
from jax import lax
from jax.sharding import PartitionSpec as P

BF16 = jnp.bfloat16
F32 = jnp.float32
GRID = ("shell", "row")


def complex_block(real_part, imag_part):
    upper_half = jnp.concatenate([real_part, imag_part], axis=1)
    lower_half = jnp.concatenate([-imag_part, real_part], axis=1)
    return jnp.concatenate([upper_half, lower_half], axis=0)


def weigh_points(right_basis, point_weight, shell_index, green_table):
    shells_count = green_table.shape[0]
    matches = shell_index[:, None] == jnp.arange(shells_count, dtype=jnp.int32)[None, :]
    green_real = jnp.sum(jnp.where(matches, green_table[None, :, 0], 0.0), axis=1)
    green_imag = jnp.sum(jnp.where(matches, green_table[None, :, 1], 0.0), axis=1)
    weight_real = point_weight * green_real
    weight_imag = point_weight * green_imag
    basis_real = right_basis[0].astype(F32)
    basis_imag = right_basis[1].astype(F32)
    weighted_real = (weight_real[:, None] * basis_real - weight_imag[:, None] * basis_imag).astype(BF16)
    weighted_imag = (weight_real[:, None] * basis_imag + weight_imag[:, None] * basis_real).astype(BF16)
    return (weighted_real, weighted_imag)


def exchange(blocks, axes):
    return lax.all_to_all(blocks, axes, 0, 0, tiled=False)


def gather_blocks(block, axes, count):
    return exchange(jnp.broadcast_to(block[None], (count,) + block.shape), axes)


def body(left_basis, right_basis, point_weight, shell_index, green_table, pivot_rows, diag_inverse):
    shells = lax.axis_size("shell")
    grid_rows = lax.axis_size("row")
    columns = lax.axis_size("col")
    holders = shells * grid_rows
    tile_rows = left_basis.shape[1]
    owned_rows = tile_rows // shells
    width = right_basis.shape[2]
    pivots_count = pivot_rows.shape[0]
    weighted_real, weighted_imag = weigh_points(right_basis, point_weight, shell_index, green_table)
    left_stack = jnp.concatenate([left_basis[0], left_basis[1]], axis=1)
    right_stack = complex_block(weighted_real, weighted_imag)
    terms = jnp.dot(left_stack, right_stack, preferred_element_type=F32).astype(BF16)

    coupling = lax.psum_scatter(terms, "shell", scatter_dimension=0, tiled=True).astype(F32)

    tile_index = lax.broadcasted_iota(jnp.int32, (pivots_count, tile_rows), 1) + lax.axis_index("row") * tile_rows
    chosen = (pivot_rows[:, None] == tile_index).astype(BF16)
    picked = jnp.dot(chosen, terms, preferred_element_type=F32).astype(BF16)
    shares = exchange(picked.reshape(holders, pivots_count // holders, 2 * width), GRID)
    pivot_share = jnp.sum(shares.astype(F32), axis=0).astype(BF16)
    pivots = gather_blocks(pivot_share, GRID, holders).reshape(pivots_count, 2 * width)

    panel_real = coupling[:, :width]
    panel_imag = coupling[:, width:]
    inverse_real = diag_inverse[0].astype(F32)
    inverse_imag = diag_inverse[1].astype(F32)
    highest = lax.Precision.HIGHEST
    mult_real = (
        jnp.dot(panel_real, inverse_real, precision=highest, preferred_element_type=F32)
        - jnp.dot(panel_imag, inverse_imag, precision=highest, preferred_element_type=F32)
    ).astype(BF16)
    mult_imag = (
        jnp.dot(panel_real, inverse_imag, precision=highest, preferred_element_type=F32)
        + jnp.dot(panel_imag, inverse_real, precision=highest, preferred_element_type=F32)
    ).astype(BF16)
    multipliers = jnp.concatenate([mult_real, mult_imag], axis=1)
    spread = exchange(multipliers.reshape(columns, owned_rows // columns, 2 * width), "col")[0]
    multipliers = gather_blocks(spread, "col", columns).reshape(owned_rows, 2 * width)

    pivot_block = complex_block(pivots[:, :width], pivots[:, width:])
    updated = coupling - jnp.dot(multipliers, pivot_block, preferred_element_type=F32)
    return jnp.stack([updated[:, :width], updated[:, width:]]).reshape(2, 1, 1, owned_rows, width)


def solution(mesh):
    return jax.shard_map(
        body,
        mesh=mesh,
        in_specs=(
            P(None, "row", "shell"),
            P(None, "shell", "col"),
            P("shell"),
            P("shell"),
            P(),
            P(),
            P(),
        ),
        out_specs=P(None, "row", "shell", None, "col"),
        check_vma=False,
    )
```

```python
import jax
import jax.numpy as jnp
from jax import lax
from jax.sharding import PartitionSpec as P

BF16 = jnp.bfloat16
F32 = jnp.float32


def weigh_points(right_basis, point_weight, shell_index, green_table):
    shells_count = green_table.shape[0]
    matches = shell_index[:, None] == jnp.arange(shells_count, dtype=jnp.int32)[None, :]
    green_real = jnp.sum(jnp.where(matches, green_table[None, :, 0], 0.0), axis=1)
    green_imag = jnp.sum(jnp.where(matches, green_table[None, :, 1], 0.0), axis=1)
    weight_real = point_weight * green_real
    weight_imag = point_weight * green_imag
    basis_real = right_basis[0].astype(F32)
    basis_imag = right_basis[1].astype(F32)
    weighted_real = (weight_real[:, None] * basis_real - weight_imag[:, None] * basis_imag).astype(BF16)
    weighted_imag = (weight_real[:, None] * basis_imag + weight_imag[:, None] * basis_real).astype(BF16)
    return (weighted_real, weighted_imag)


def exchange(blocks, axes):
    return lax.all_to_all(blocks, axes, 0, 0, tiled=False)


def dot(a, b):
    return jnp.dot(a, b, preferred_element_type=F32)


def swap(block, bit):
    count = lax.axis_size("row")
    return lax.ppermute(block, "row", [(i, i ^ bit) for i in range(count)])


def pick(blocks, index, axis):
    return lax.dynamic_index_in_dim(blocks, index, axis, keepdims=False)


def ordered(mine, theirs, side):
    return jnp.where(side == 0, jnp.stack([mine, theirs]), jnp.stack([theirs, mine]))


def complex_block(real_part, imag_part):
    upper_half = jnp.concatenate([real_part, imag_part], axis=1)
    lower_half = jnp.concatenate([-imag_part, real_part], axis=1)
    return jnp.concatenate([upper_half, lower_half], axis=0)


def forward(value, sends):
    arrived = [lax.ppermute(value, "col", pairs) for pairs in sends]
    return value + arrived[0] + arrived[1] + arrived[2]


FIRST_SENDS = (((0, 8),), ((0, 2),), ((0, 6),))
SECOND_SENDS = (
    ((0, 1), (8, 9), (2, 10), (6, 14)),
    ((0, 7), (8, 15), (2, 3), (6, 5)),
    ((0, 4), (8, 12), (2, 11), (6, 13)),
)


def body(left_basis, right_basis, point_weight, shell_index, green_table, pivot_rows, diag_inverse):
    shells = lax.axis_size("shell")
    tile_rows = left_basis.shape[1]
    owned_rows = tile_rows // shells
    width = right_basis.shape[2]
    pivots_count = pivot_rows.shape[0]
    grid_row = lax.axis_index("row")
    core, chip = grid_row % 2, grid_row // 2
    weighted_real, weighted_imag = weigh_points(right_basis, point_weight, shell_index, green_table)
    left_stack = jnp.concatenate([left_basis[0], left_basis[1]], axis=1)
    terms = dot(left_stack, complex_block(weighted_real, weighted_imag)).astype(BF16)
    tile_sums = lax.psum_scatter(terms, "shell", scatter_dimension=0, tiled=True)

    tile_index = lax.broadcasted_iota(jnp.int32, (pivots_count, tile_rows), 1) + grid_row * tile_rows
    chosen = (pivot_rows[:, None] == tile_index).astype(BF16)
    picked = dot(chosen, terms).astype(BF16)
    picked = picked.reshape(2, pivots_count // 2, 2 * width)
    picked = pick(picked, core, 0) + swap(pick(picked, 1 - core, 0), 1)
    share_rows = pivots_count // (4 * shells)
    picked = picked.reshape(shells, 2, share_rows, 2 * width)
    picked = pick(picked, chip, 1) + swap(pick(picked, 1 - chip, 1), 2)
    shares = exchange(picked, "shell")
    share = jnp.sum(shares.astype(F32), axis=0).astype(BF16)
    pair = ordered(share, swap(share, 2), chip)
    half = exchange(jnp.broadcast_to(pair[None], (shells,) + pair.shape), "shell").reshape(pivots_count // 2, 2 * width)
    panel = jnp.where(lax.axis_index("col") == 0, tile_sums, jnp.zeros_like(tile_sums))
    panel = forward(panel, FIRST_SENDS)
    half, panel = lax.optimization_barrier((half, panel))
    panel = forward(panel, SECOND_SENDS)
    pivots = jnp.concatenate([half, swap(half, 1)], axis=0)

    side = pivots_count // 2
    turned = jnp.concatenate([diag_inverse[:, :, side:], diag_inverse[:, :, :side]], axis=2)
    inverse = jnp.where(core == 0, diag_inverse, turned)
    inverse_block = jnp.concatenate([inverse[0], inverse[1]], axis=1)
    solved = dot(
        inverse_block,
        jnp.concatenate(
            [pivots, jnp.concatenate([-pivots[:, width:], pivots[:, :width]], axis=1)],
            axis=0,
        ),
    )
    coarse = lax.reduce_precision(solved, 8, 7)
    fine = (solved - coarse).astype(BF16)
    coarse = coarse.astype(BF16)
    turn = lambda block: jnp.concatenate([-block[:, width:], block[:, :width]], axis=1)
    updated = tile_sums.astype(F32) - dot(
        jnp.concatenate([panel, panel], axis=1),
        jnp.concatenate([coarse, turn(coarse), fine, turn(fine)], axis=0),
    )
    return jnp.stack([updated[:, :width], updated[:, width:]]).reshape(2, 1, 1, owned_rows, width)


def solution(mesh):
    return jax.shard_map(
        body,
        mesh=mesh,
        in_specs=(
            P(None, "row", "shell"),
            P(None, "shell", "col"),
            P("shell"),
            P("shell"),
            P(),
            P(),
            P(),
        ),
        out_specs=P(None, "row", "shell", None, "col"),
        check_vma=False,
    )
```

```python
import jax
import jax.numpy as jnp
from jax import lax
from jax.experimental import pallas as pl
from jax.experimental.pallas import tpu as pltpu
from jax.sharding import PartitionSpec as P

BF16 = jnp.bfloat16
F32 = jnp.float32


LANES = 128
SUBLANES = 8
ROW_STEPS = 4


def terms_kernel(
    green_ref, weight_ref, index_ref, left_hbm, right_hbm, terms_hbm,
    left_ref, right_ref, stack_ref, terms_ref, in_sems, out_sems,
):
    points, width = right_ref.shape[1], right_ref.shape[2]
    right_copy = pltpu.make_async_copy(right_hbm, right_ref, in_sems.at[0])
    left_copy = pltpu.make_async_copy(left_hbm, left_ref, in_sems.at[1])
    right_copy.start()
    left_copy.start()

    index = index_ref[...]
    green_real = jnp.zeros(index.shape, F32)
    green_imag = jnp.zeros(index.shape, F32)
    for shell in range(green_ref.shape[1]):
        match = index == shell
        green_real = jnp.where(match, green_ref[0, shell], green_real)
        green_imag = jnp.where(match, green_ref[1, shell], green_imag)
    groups = index.shape[0]
    fill = jnp.zeros((-groups % SUBLANES, LANES), F32)
    weight_real = jnp.transpose(jnp.concatenate([weight_ref[...] * green_real, fill], axis=0))
    weight_imag = jnp.transpose(jnp.concatenate([weight_ref[...] * green_imag, fill], axis=0))
    right_copy.wait()
    for group in range(groups):
        rows = slice(group * LANES, (group + 1) * LANES)
        below = slice(points + group * LANES, points + (group + 1) * LANES)
        factor_real = weight_real[:, group : group + 1]
        factor_imag = weight_imag[:, group : group + 1]
        basis_real = right_ref[0, rows, :].astype(F32)
        basis_imag = right_ref[1, rows, :].astype(F32)
        real = (factor_real * basis_real - factor_imag * basis_imag).astype(BF16)
        imag = (factor_real * basis_imag + factor_imag * basis_real).astype(BF16)
        stack_ref[rows, :width] = real
        stack_ref[rows, width:] = imag
        stack_ref[below, :width] = -imag
        stack_ref[below, width:] = real

    left_copy.wait()
    step_rows = left_ref.shape[1] // ROW_STEPS
    copies = []
    for step in range(ROW_STEPS):
        rows = slice(step * step_rows, (step + 1) * step_rows)
        total = jnp.dot(left_ref[0, rows, :], stack_ref[:points, :], preferred_element_type=F32)
        total = total + jnp.dot(left_ref[1, rows, :], stack_ref[points:, :], preferred_element_type=F32)
        terms_ref[rows, :] = total.astype(BF16)
        copy = pltpu.make_async_copy(
            terms_ref.at[pl.ds(step * step_rows, step_rows), :],
            terms_hbm.at[pl.ds(step * step_rows, step_rows), :],
            out_sems.at[step],
        )
        copy.start()
        copies.append(copy)
    for copy in copies:
        copy.wait()


def partial_terms(left_basis, right_basis, point_weight, shell_index, green_table):
    _, tile_rows, points = left_basis.shape
    width = right_basis.shape[2]
    groups = points // LANES
    in_vmem = pl.BlockSpec(memory_space=pltpu.VMEM)
    in_hbm = pl.BlockSpec(memory_space=pltpu.HBM)
    return pl.pallas_call(
        terms_kernel,
        in_specs=[pl.BlockSpec(memory_space=pltpu.SMEM), in_vmem, in_vmem, in_hbm, in_hbm],
        out_specs=in_hbm,
        out_shape=jax.ShapeDtypeStruct((tile_rows, 2 * width), BF16),
        scratch_shapes=[
            pltpu.VMEM(left_basis.shape, BF16),
            pltpu.VMEM(right_basis.shape, BF16),
            pltpu.VMEM((2 * points, 2 * width), BF16),
            pltpu.VMEM((tile_rows, 2 * width), BF16),
            pltpu.SemaphoreType.DMA((2,)),
            pltpu.SemaphoreType.DMA((ROW_STEPS,)),
        ],
        compiler_params=pltpu.CompilerParams(vmem_limit_bytes=62 * 1024 * 1024),
        cost_estimate=pl.CostEstimate(
            flops=8 * tile_rows * points * width,
            transcendentals=0,
            bytes_accessed=2 * (left_basis.size + right_basis.size + 2 * tile_rows * width),
        ),
        name="terms",
    )(
        green_table.T,
        point_weight.reshape(groups, LANES),
        shell_index.reshape(groups, LANES),
        left_basis,
        right_basis,
    )


def exchange(blocks, axes):
    return lax.all_to_all(blocks, axes, 0, 0, tiled=False)


def dot(a, b):
    return jnp.dot(a, b, preferred_element_type=F32)


def swap(block, bit):
    count = lax.axis_size("row")
    return lax.ppermute(block, "row", [(i, i ^ bit) for i in range(count)])


def pick(blocks, index, axis):
    return lax.dynamic_index_in_dim(blocks, index, axis, keepdims=False)


def ordered(mine, theirs, side):
    return jnp.where(side == 0, jnp.stack([mine, theirs]), jnp.stack([theirs, mine]))


def forward(value, sends):
    arrived = [lax.ppermute(value, "col", pairs) for pairs in sends]
    return value + arrived[0] + arrived[1] + arrived[2]


FIRST_SENDS = (((0, 8),), ((0, 2),), ((0, 6),))
SECOND_SENDS = (
    ((0, 9), (8, 11), (2, 4), (6, 12)),
    ((0, 7), (8, 13), (2, 10), (6, 14)),
    ((0, 1), (8, 15), (2, 3), (6, 5)),
)


def body(left_basis, right_basis, point_weight, shell_index, green_table, pivot_rows, diag_inverse):
    shells = lax.axis_size("shell")
    tile_rows = left_basis.shape[1]
    owned_rows = tile_rows // shells
    width = right_basis.shape[2]
    pivots_count = pivot_rows.shape[0]
    grid_row = lax.axis_index("row")
    core, chip = grid_row % 2, grid_row // 2
    terms = partial_terms(left_basis, right_basis, point_weight, shell_index, green_table)
    tile_sums = lax.psum_scatter(terms, "shell", scatter_dimension=0, tiled=True)

    tile_index = lax.broadcasted_iota(jnp.int32, (pivots_count, tile_rows), 1) + grid_row * tile_rows
    chosen = (pivot_rows[:, None] == tile_index).astype(BF16)
    picked = dot(chosen, terms).astype(BF16)
    picked = picked.reshape(2, pivots_count // 2, 2 * width)
    picked = pick(picked, core, 0) + swap(pick(picked, 1 - core, 0), 1)
    share_rows = pivots_count // (4 * shells)
    picked = picked.reshape(shells, 2, share_rows, 2 * width)
    picked = pick(picked, chip, 1) + swap(pick(picked, 1 - chip, 1), 2)
    shares = exchange(picked, "shell")
    share = jnp.sum(shares.astype(F32), axis=0).astype(BF16)
    pair = ordered(share, swap(share, 2), chip)
    half = exchange(jnp.broadcast_to(pair[None], (shells,) + pair.shape), "shell").reshape(pivots_count // 2, 2 * width)
    panel = jnp.where(lax.axis_index("col") == 0, tile_sums, jnp.zeros_like(tile_sums))
    panel = forward(panel, FIRST_SENDS)
    half, _ = lax.optimization_barrier((half, panel))
    panel = forward(panel, SECOND_SENDS)
    pivots = jnp.concatenate([half, swap(half, 1)], axis=0)

    side = pivots_count // 2
    turned = jnp.concatenate([diag_inverse[:, :, side:], diag_inverse[:, :, :side]], axis=2)
    inverse = jnp.where(core == 0, diag_inverse, turned)
    inverse_block = jnp.concatenate([inverse[0], inverse[1]], axis=1)
    solved = dot(
        inverse_block,
        jnp.concatenate(
            [pivots, jnp.concatenate([-pivots[:, width:], pivots[:, :width]], axis=1)],
            axis=0,
        ),
    )
    coarse = lax.reduce_precision(solved, 8, 7)
    fine = (solved - coarse).astype(BF16)
    coarse = coarse.astype(BF16)
    turn = lambda block: jnp.concatenate([-block[:, width:], block[:, :width]], axis=1)
    updated = tile_sums.astype(F32) - dot(
        jnp.concatenate([panel, panel], axis=1),
        jnp.concatenate([coarse, turn(coarse), fine, turn(fine)], axis=0),
    )
    return jnp.stack([updated[:, :width], updated[:, width:]]).reshape(2, 1, 1, owned_rows, width)


def solution(mesh):
    return jax.shard_map(
        body,
        mesh=mesh,
        in_specs=(
            P(None, "row", "shell"),
            P(None, "shell", "col"),
            P("shell"),
            P("shell"),
            P(),
            P(),
            P(),
        ),
        out_specs=P(None, "row", "shell", None, "col"),
        check_vma=False,
    )
```

```python
import jax
import jax.numpy as jnp
from jax import lax
from jax.experimental import pallas as pl
from jax.experimental.pallas import tpu as pltpu
from jax.sharding import PartitionSpec as P

BF16 = jnp.bfloat16
F32 = jnp.float32


LANES = 128
SUBLANES = 8
ROW_STEPS = 4


def terms_kernel(
    green_ref, weight_ref, index_ref, pivot_ref, left_hbm, right_hbm, terms_hbm, send_hbm, keep_hbm,
    left_ref, right_ref, stack_ref, terms_ref, picked_ref, in_sems, out_sems, picked_sems,
):
    points, width = right_ref.shape[1], right_ref.shape[2]
    right_copy = pltpu.make_async_copy(right_hbm, right_ref, in_sems.at[0])
    left_copy = pltpu.make_async_copy(left_hbm, left_ref, in_sems.at[1])
    right_copy.start()
    left_copy.start()

    index = index_ref[...]
    green_real = jnp.zeros(index.shape, F32)
    green_imag = jnp.zeros(index.shape, F32)
    for shell in range(green_ref.shape[1]):
        match = index == shell
        green_real = jnp.where(match, green_ref[0, shell], green_real)
        green_imag = jnp.where(match, green_ref[1, shell], green_imag)
    groups = index.shape[0]
    fill = jnp.zeros((-groups % SUBLANES, LANES), F32)
    weight_real = jnp.transpose(jnp.concatenate([weight_ref[...] * green_real, fill], axis=0))
    weight_imag = jnp.transpose(jnp.concatenate([weight_ref[...] * green_imag, fill], axis=0))
    right_copy.wait()
    for group in range(groups):
        rows = slice(group * LANES, (group + 1) * LANES)
        below = slice(points + group * LANES, points + (group + 1) * LANES)
        factor_real = weight_real[:, group : group + 1]
        factor_imag = weight_imag[:, group : group + 1]
        basis_real = right_ref[0, rows, :].astype(F32)
        basis_imag = right_ref[1, rows, :].astype(F32)
        real = (factor_real * basis_real - factor_imag * basis_imag).astype(BF16)
        imag = (factor_real * basis_imag + factor_imag * basis_real).astype(BF16)
        stack_ref[rows, :width] = real
        stack_ref[rows, width:] = imag
        stack_ref[below, :width] = -imag
        stack_ref[below, width:] = real

    left_copy.wait()
    step_rows = left_ref.shape[1] // ROW_STEPS
    copies = []
    for step in range(ROW_STEPS):
        rows = slice(step * step_rows, (step + 1) * step_rows)
        total = jnp.dot(left_ref[0, rows, :], stack_ref[:points, :], preferred_element_type=F32)
        total = total + jnp.dot(left_ref[1, rows, :], stack_ref[points:, :], preferred_element_type=F32)
        terms_ref[rows, :] = total.astype(BF16)
        copy = pltpu.make_async_copy(
            terms_ref.at[pl.ds(step * step_rows, step_rows), :],
            terms_hbm.at[pl.ds(step * step_rows, step_rows), :],
            out_sems.at[step],
        )
        copy.start()
        copies.append(copy)

    grid_row = lax.axis_index("row")
    core = grid_row % 2
    tile_rows = terms_ref.shape[0]
    pivot_groups = pivot_ref.shape[0]
    pivot_fill = jnp.zeros((-pivot_groups % SUBLANES, LANES), jnp.int32)
    local = jnp.transpose(jnp.concatenate([pivot_ref[...] - grid_row * tile_rows, pivot_fill], axis=0))
    row_index = lax.broadcasted_iota(jnp.int32, (LANES, tile_rows), 1)
    side = pivot_groups // 2
    for part, picked_hbm in enumerate((send_hbm, keep_hbm)):
        for group in range(side):
            low, high = local[:, group : group + 1], local[:, side + group : side + group + 1]
            wanted = jnp.where(core == (1 - part), low, high)
            chosen = jnp.where(row_index == wanted, 1.0, 0.0).astype(BF16)
            rows = slice(group * LANES, (group + 1) * LANES)
            picked = jnp.dot(chosen, terms_ref[...], preferred_element_type=F32)
            picked_ref[part, rows, :] = picked.astype(BF16)
        copy = pltpu.make_async_copy(picked_ref.at[part], picked_hbm, picked_sems.at[part])
        copy.start()
        copies.append(copy)
    for copy in copies:
        copy.wait()


def partial_terms(left_basis, right_basis, point_weight, shell_index, green_table, pivot_rows):
    _, tile_rows, points = left_basis.shape
    width = right_basis.shape[2]
    groups = points // LANES
    pivots_count = pivot_rows.shape[0]
    in_vmem = pl.BlockSpec(memory_space=pltpu.VMEM)
    in_hbm = pl.BlockSpec(memory_space=pltpu.HBM)
    return pl.pallas_call(
        terms_kernel,
        in_specs=[pl.BlockSpec(memory_space=pltpu.SMEM), in_vmem, in_vmem, in_vmem, in_hbm, in_hbm],
        out_specs=[in_hbm] * 3,
        out_shape=[jax.ShapeDtypeStruct((tile_rows, 2 * width), BF16)]
        + [jax.ShapeDtypeStruct((pivots_count // 2, 2 * width), BF16)] * 2,
        scratch_shapes=[
            pltpu.VMEM(left_basis.shape, BF16),
            pltpu.VMEM(right_basis.shape, BF16),
            pltpu.VMEM((2 * points, 2 * width), BF16),
            pltpu.VMEM((tile_rows, 2 * width), BF16),
            pltpu.VMEM((2, pivots_count // 2, 2 * width), BF16),
            pltpu.SemaphoreType.DMA((2,)),
            pltpu.SemaphoreType.DMA((ROW_STEPS,)),
            pltpu.SemaphoreType.DMA((2,)),
        ],
        compiler_params=pltpu.CompilerParams(vmem_limit_bytes=62 * 1024 * 1024),
        cost_estimate=pl.CostEstimate(
            flops=8 * tile_rows * points * width + 4 * pivots_count * tile_rows * width,
            transcendentals=0,
            bytes_accessed=2 * (left_basis.size + right_basis.size + 2 * tile_rows * width),
        ),
        name="terms",
    )(
        green_table.T,
        point_weight.reshape(groups, LANES),
        shell_index.reshape(groups, LANES),
        pivot_rows.reshape(pivots_count // LANES, LANES),
        left_basis,
        right_basis,
    )


def exchange(blocks, axes):
    return lax.all_to_all(blocks, axes, 0, 0, tiled=False)


def dot(a, b):
    return jnp.dot(a, b, preferred_element_type=F32)


def swap(block, bit):
    count = lax.axis_size("row")
    return lax.ppermute(block, "row", [(i, i ^ bit) for i in range(count)])


def pick(blocks, index, axis):
    return lax.dynamic_index_in_dim(blocks, index, axis, keepdims=False)


def ordered(mine, theirs, side):
    return jnp.where(side == 0, jnp.stack([mine, theirs]), jnp.stack([theirs, mine]))


def forward(value, sends):
    arrived = [lax.ppermute(value, "col", pairs) for pairs in sends]
    return value + arrived[0] + arrived[1] + arrived[2]


FIRST_SENDS = (((0, 8),), ((0, 2),), ((0, 6),))
SECOND_SENDS = (
    ((0, 9), (8, 11), (2, 4), (6, 12)),
    ((0, 7), (8, 13), (2, 10), (6, 14)),
    ((0, 1), (8, 15), (2, 3), (6, 5)),
)


def body(left_basis, right_basis, point_weight, shell_index, green_table, pivot_rows, diag_inverse):
    shells = lax.axis_size("shell")
    tile_rows = left_basis.shape[1]
    owned_rows = tile_rows // shells
    width = right_basis.shape[2]
    pivots_count = pivot_rows.shape[0]
    grid_row = lax.axis_index("row")
    core, chip = grid_row % 2, grid_row // 2
    terms, passed, kept = partial_terms(
        left_basis, right_basis, point_weight, shell_index, green_table, pivot_rows
    )
    tile_sums = lax.psum_scatter(terms, "shell", scatter_dimension=0, tiled=True)

    picked = kept + swap(passed, 1)
    share_rows = pivots_count // (4 * shells)
    picked = picked.reshape(shells, 2, share_rows, 2 * width)
    picked = pick(picked, chip, 1) + swap(pick(picked, 1 - chip, 1), 2)
    shares = exchange(picked, "shell")
    share = jnp.sum(shares.astype(F32), axis=0).astype(BF16)
    pair = ordered(share, swap(share, 2), chip)
    half = exchange(jnp.broadcast_to(pair[None], (shells,) + pair.shape), "shell").reshape(pivots_count // 2, 2 * width)
    first = [lax.ppermute(tile_sums, "col", pairs) for pairs in FIRST_SENDS]
    panel = jnp.where(lax.axis_index("col") == 0, tile_sums, first[0] + first[1] + first[2])
    half, _ = lax.optimization_barrier((half, panel))
    panel = forward(panel, SECOND_SENDS)
    pivots = jnp.concatenate([half, swap(half, 1)], axis=0)

    side = pivots_count // 2
    turned = jnp.concatenate([diag_inverse[:, :, side:], diag_inverse[:, :, :side]], axis=2)
    inverse = jnp.where(core == 0, diag_inverse, turned)
    inverse_block = jnp.concatenate([inverse[0], inverse[1]], axis=1)
    solved = dot(
        inverse_block,
        jnp.concatenate(
            [pivots, jnp.concatenate([-pivots[:, width:], pivots[:, :width]], axis=1)],
            axis=0,
        ),
    )
    coarse = lax.reduce_precision(solved, 8, 7)
    fine = (solved - coarse).astype(BF16)
    coarse = coarse.astype(BF16)
    turn = lambda block: jnp.concatenate([-block[:, width:], block[:, :width]], axis=1)
    updated = tile_sums.astype(F32) - dot(
        jnp.concatenate([panel, panel], axis=1),
        jnp.concatenate([coarse, turn(coarse), fine, turn(fine)], axis=0),
    )
    return jnp.stack([updated[:, :width], updated[:, width:]]).reshape(2, 1, 1, owned_rows, width)


def solution(mesh):
    return jax.shard_map(
        body,
        mesh=mesh,
        in_specs=(
            P(None, "row", "shell"),
            P(None, "shell", "col"),
            P("shell"),
            P("shell"),
            P(),
            P(),
            P(),
        ),
        out_specs=P(None, "row", "shell", None, "col"),
        check_vma=False,
    )
```

```python
import jax
import jax.numpy as jnp
from jax import lax
from jax.experimental import pallas as pl
from jax.experimental.pallas import tpu as pltpu
from jax.sharding import PartitionSpec as P

BF16 = jnp.bfloat16
F32 = jnp.float32


LANES = 128
SUBLANES = 8
ROW_STEPS = 4


def terms_kernel(
    green_ref, weight_ref, index_ref, pivot_ref, left_hbm, right_hbm, terms_hbm, send_hbm, keep_hbm,
    left_ref, right_ref, stack_ref, terms_ref, picked_ref, in_sems, out_sems, picked_sems,
):
    points, width = right_ref.shape[1], right_ref.shape[2]
    right_copy = pltpu.make_async_copy(right_hbm, right_ref, in_sems.at[0])
    left_copy = pltpu.make_async_copy(left_hbm, left_ref, in_sems.at[1])
    right_copy.start()
    left_copy.start()

    index = index_ref[...]
    green_real = jnp.zeros(index.shape, F32)
    green_imag = jnp.zeros(index.shape, F32)
    for shell in range(green_ref.shape[1]):
        match = index == shell
        green_real = jnp.where(match, green_ref[0, shell], green_real)
        green_imag = jnp.where(match, green_ref[1, shell], green_imag)
    groups = index.shape[0]
    fill = jnp.zeros((-groups % SUBLANES, LANES), F32)
    weight_real = jnp.transpose(jnp.concatenate([weight_ref[...] * green_real, fill], axis=0))
    weight_imag = jnp.transpose(jnp.concatenate([weight_ref[...] * green_imag, fill], axis=0))
    right_copy.wait()
    for group in range(groups):
        rows = slice(group * LANES, (group + 1) * LANES)
        below = slice(points + group * LANES, points + (group + 1) * LANES)
        factor_real = weight_real[:, group : group + 1]
        factor_imag = weight_imag[:, group : group + 1]
        basis_real = right_ref[0, rows, :].astype(F32)
        basis_imag = right_ref[1, rows, :].astype(F32)
        real = (factor_real * basis_real - factor_imag * basis_imag).astype(BF16)
        imag = (factor_real * basis_imag + factor_imag * basis_real).astype(BF16)
        stack_ref[rows, :width] = real
        stack_ref[rows, width:] = imag
        stack_ref[below, :width] = -imag
        stack_ref[below, width:] = real

    left_copy.wait()
    step_rows = left_ref.shape[1] // ROW_STEPS
    copies = []
    for step in range(ROW_STEPS):
        rows = slice(step * step_rows, (step + 1) * step_rows)
        total = jnp.dot(left_ref[0, rows, :], stack_ref[:points, :], preferred_element_type=F32)
        total = total + jnp.dot(left_ref[1, rows, :], stack_ref[points:, :], preferred_element_type=F32)
        terms_ref[rows, :] = total.astype(BF16)
        copy = pltpu.make_async_copy(
            terms_ref.at[pl.ds(step * step_rows, step_rows), :],
            terms_hbm.at[pl.ds(step * step_rows, step_rows), :],
            out_sems.at[step],
        )
        copy.start()
        copies.append(copy)

    grid_row = lax.axis_index("row")
    core = grid_row % 2
    tile_rows = terms_ref.shape[0]
    pivot_groups = pivot_ref.shape[0]
    pivot_fill = jnp.zeros((-pivot_groups % SUBLANES, LANES), jnp.int32)
    local = jnp.transpose(jnp.concatenate([pivot_ref[...] - grid_row * tile_rows, pivot_fill], axis=0))
    row_index = lax.broadcasted_iota(jnp.int32, (LANES, tile_rows), 1)
    side = pivot_groups // 2
    for part, picked_hbm in enumerate((send_hbm, keep_hbm)):
        for group in range(side):
            low, high = local[:, group : group + 1], local[:, side + group : side + group + 1]
            wanted = jnp.where(core == (1 - part), low, high)
            chosen = jnp.where(row_index == wanted, 1.0, 0.0).astype(BF16)
            rows = slice(group * LANES, (group + 1) * LANES)
            picked = jnp.dot(chosen, terms_ref[...], preferred_element_type=F32)
            picked_ref[part, rows, :] = picked.astype(BF16)
        copy = pltpu.make_async_copy(picked_ref.at[part], picked_hbm, picked_sems.at[part])
        copy.start()
        copies.append(copy)
    for copy in copies:
        copy.wait()


def partial_terms(left_basis, right_basis, point_weight, shell_index, green_table, pivot_rows):
    _, tile_rows, points = left_basis.shape
    width = right_basis.shape[2]
    groups = points // LANES
    pivots_count = pivot_rows.shape[0]
    in_vmem = pl.BlockSpec(memory_space=pltpu.VMEM)
    in_hbm = pl.BlockSpec(memory_space=pltpu.HBM)
    return pl.pallas_call(
        terms_kernel,
        in_specs=[pl.BlockSpec(memory_space=pltpu.SMEM), in_vmem, in_vmem, in_vmem, in_hbm, in_hbm],
        out_specs=[in_hbm] * 3,
        out_shape=[jax.ShapeDtypeStruct((tile_rows, 2 * width), BF16)]
        + [jax.ShapeDtypeStruct((pivots_count // 2, 2 * width), BF16)] * 2,
        scratch_shapes=[
            pltpu.VMEM(left_basis.shape, BF16),
            pltpu.VMEM(right_basis.shape, BF16),
            pltpu.VMEM((2 * points, 2 * width), BF16),
            pltpu.VMEM((tile_rows, 2 * width), BF16),
            pltpu.VMEM((2, pivots_count // 2, 2 * width), BF16),
            pltpu.SemaphoreType.DMA((2,)),
            pltpu.SemaphoreType.DMA((ROW_STEPS,)),
            pltpu.SemaphoreType.DMA((2,)),
        ],
        compiler_params=pltpu.CompilerParams(vmem_limit_bytes=62 * 1024 * 1024),
        cost_estimate=pl.CostEstimate(
            flops=8 * tile_rows * points * width + 4 * pivots_count * tile_rows * width,
            transcendentals=0,
            bytes_accessed=2 * (left_basis.size + right_basis.size + 2 * tile_rows * width),
        ),
        name="terms",
    )(
        green_table.T,
        point_weight.reshape(groups, LANES),
        shell_index.reshape(groups, LANES),
        pivot_rows.reshape(pivots_count // LANES, LANES),
        left_basis,
        right_basis,
    )


def exchange(blocks, axes):
    return lax.all_to_all(blocks, axes, 0, 0, tiled=False)


def dot(a, b):
    return jnp.dot(a, b, preferred_element_type=F32)


def swap(block, bit):
    count = lax.axis_size("row")
    return lax.ppermute(block, "row", [(i, i ^ bit) for i in range(count)])


def pick(blocks, index, axis):
    return lax.dynamic_index_in_dim(blocks, index, axis, keepdims=False)


def ordered(mine, theirs, side):
    return jnp.where(side == 0, jnp.stack([mine, theirs]), jnp.stack([theirs, mine]))


def forward(value, sends):
    arrived = [lax.ppermute(value, "col", pairs) for pairs in sends]
    return value + arrived[0] + arrived[1] + arrived[2]


FIRST_SENDS = (((0, 8),), ((0, 2),), ((0, 6),))
SECOND_SENDS = (
    ((0, 9), (8, 11), (2, 4), (6, 12)),
    ((0, 7), (8, 13), (2, 10), (6, 14)),
    ((0, 1), (8, 15), (2, 3), (6, 5)),
)


def body(left_basis, right_basis, point_weight, shell_index, green_table, pivot_rows, diag_inverse):
    shells = lax.axis_size("shell")
    tile_rows = left_basis.shape[1]
    owned_rows = tile_rows // shells
    width = right_basis.shape[2]
    pivots_count = pivot_rows.shape[0]
    grid_row = lax.axis_index("row")
    core, chip = grid_row % 2, grid_row // 2
    terms, passed, kept = partial_terms(
        left_basis, right_basis, point_weight, shell_index, green_table, pivot_rows
    )
    tile_sums = lax.psum_scatter(terms, "shell", scatter_dimension=0, tiled=True)

    share_rows = pivots_count // (4 * shells)
    kept = kept.reshape(shells, 2, share_rows, 2 * width)
    got = swap(passed, 1).reshape(kept.shape)
    leaving = pick(kept, 1 - chip, 1) + pick(got, 1 - chip, 1)
    picked = pick(kept, chip, 1) + pick(got, chip, 1) + swap(leaving, 2)
    shares = exchange(picked, "shell")
    share = jnp.sum(shares.astype(F32), axis=0).astype(BF16)
    pair = ordered(share, swap(share, 2), chip)
    half = exchange(jnp.broadcast_to(pair[None], (shells,) + pair.shape), "shell").reshape(pivots_count // 2, 2 * width)
    first = [lax.ppermute(tile_sums, "col", pairs) for pairs in FIRST_SENDS]
    panel = jnp.where(lax.axis_index("col") == 0, tile_sums, first[0] + first[1] + first[2])
    half, _ = lax.optimization_barrier((half, panel))
    panel = forward(panel, SECOND_SENDS)
    pivots = jnp.concatenate([half, swap(half, 1)], axis=0)

    side = pivots_count // 2
    turned = jnp.concatenate([diag_inverse[:, :, side:], diag_inverse[:, :, :side]], axis=2)
    inverse = jnp.where(core == 0, diag_inverse, turned)
    inverse_block = jnp.concatenate([inverse[0], inverse[1]], axis=1)
    solved = dot(
        inverse_block,
        jnp.concatenate(
            [pivots, jnp.concatenate([-pivots[:, width:], pivots[:, :width]], axis=1)],
            axis=0,
        ),
    )
    coarse = lax.reduce_precision(solved, 8, 7)
    fine = (solved - coarse).astype(BF16)
    coarse = coarse.astype(BF16)
    turn = lambda block: jnp.concatenate([-block[:, width:], block[:, :width]], axis=1)
    updated = tile_sums.astype(F32) - dot(
        jnp.concatenate([panel, panel], axis=1),
        jnp.concatenate([coarse, turn(coarse), fine, turn(fine)], axis=0),
    )
    return jnp.stack([updated[:, :width], updated[:, width:]]).reshape(2, 1, 1, owned_rows, width)


def solution(mesh):
    return jax.shard_map(
        body,
        mesh=mesh,
        in_specs=(
            P(None, "row", "shell"),
            P(None, "shell", "col"),
            P("shell"),
            P("shell"),
            P(),
            P(),
            P(),
        ),
        out_specs=P(None, "row", "shell", None, "col"),
        check_vma=False,
    )
```
